256 devices in a mesh: ctx: 64 (over x, z, core), head: 4 (over y).
Axes of the slice: x: 4, y: 4, z: 8, core: 2. Of those that a mesh axis runs over, the one named last changes fastest.
Arguments:
- queries: bfloat16 [512, 5120], P(None, 'head'), may hold values from -18 to 18
- keys: bfloat16 [32768, 1024], P('ctx', 'head'), may hold values from -20 to 20
- values: bfloat16 [32768, 1024], P('ctx', 'head'), may hold values from -6 to 6
- stretch_lengths: int32 [256], replicated, may hold values from 1 to 512, 32768 in all
- query_pos: int32 [512], replicated, may hold values from 0 to 511, each once
Outputs:
- attended: bfloat16 [512, 5120], P('ctx', 'head')
- stretch_mass: float32 [256, 512], replicated
The draws below stay inside these ranges and needn't reach their ends.
Inputs may be any that keep to these rules, and one draw needn't show every extreme that they name: `stretch_lengths`: stretch lengths sum to 32768; the longest is exactly 512. `query_pos`: each of 0 to 511 appears once.
All inputs are finite; a program needn't handle non-finite values.
Results may differ from the reference program's by a relative error of at most 0.0076.
Values sent between devices are 32-bit elements; how exact they have to be, the bound alone decides.
A program may use at most 64 MiB of HBM per device.

```python
import math
import jax
import jax.numpy as jnp
import numpy as np
from jax import lax

HQ = 40
KVH = 8
HD = 128
NQ = 512
TOK_DEV = 512
CTX_TOK = 32768
NCH = 256


def draw_queries(key, part):
    width = HQ * HD
    base = jnp.clip(3.0 * jax.random.normal(key, (NQ, width), jnp.float32), -18.0, 18.0)
    return base.astype(jnp.bfloat16)


def draw_keys(key, part):
    width = KVH * HD
    key_base = jax.random.fold_in(key, 0)
    base = jnp.clip(jax.random.normal(key_base, (CTX_TOK, width), jnp.float32), -6.0, 6.0)
    return base.astype(jnp.bfloat16)


def shard_levels(rng, dims, cuts, low, high):
    level, own = 1.0, jax.random.fold_in(rng, 6)
    for dim, parts in cuts:
        draws = jnp.exp(jax.random.uniform(jax.random.fold_in(own, dim), (parts,), jnp.float32, low / len(cuts), high / len(cuts)))
        level = level * jnp.repeat(draws, dims[dim] // parts).reshape([-1 if axis == dim else 1 for axis in range(len(dims))])
    return level


def split_up(amount, total, reach, skew):
    weights = [(1 << 20) // math.isqrt(rank ** skew) + 1 for rank in range(2, amount + 1)]
    rest, given = total - reach - (amount - 1), [1] * (amount - 1)
    while rest > 0:
        movable = [i for i in range(amount - 1) if given[i] < reach]
        mass, remaining = sum([weights[i] for i in movable]), rest
        for i in movable:
            extra = min(reach - given[i], max(1, remaining * weights[i] // mass), rest)
            given[i] = given[i] + extra
            rest = rest - extra
    return np.array([reach] + given)


def ragged(own_key, amount, total, bound, lean):
    if amount == 2:
        one = jax.random.randint(own_key, (), max(1, total - bound), min(bound, total - 1) + 1)
        return jnp.stack([one, total - one])
    sizes = jnp.asarray(split_up(amount, total, bound, lean), jnp.int32)
    twos = (amount - 1) // 2
    source_of, receiver = sizes[1:1 + 2 * twos:2], sizes[2:2 + 2 * twos:2]
    margin = jnp.minimum(source_of - 1, bound - receiver)
    passed = jax.random.randint(jax.random.fold_in(own_key, 1), (twos,), 0, 1 << 20) % (margin + 1)
    sizes = sizes.at[1:1 + 2 * twos:2].set(source_of - passed).at[2:2 + 2 * twos:2].set(receiver + passed)
    return sizes[jax.random.permutation(jax.random.fold_in(own_key, 2), amount)]


def bell_draw(stream_key, shape, spread, bound, cuts=(), kind=jnp.bfloat16):
    array = jax.random.normal(stream_key, shape, jnp.float32) * spread
    if len(cuts) > 0:
        array = shard_levels(stream_key, shape, cuts, -0.22, 0.18) * array
    return jnp.clip(array, min=-bound, max=bound).astype(kind)


def setup_inputs(seed: int = 0) -> dict:
    arg_keys = jax.random.split(jax.random.key(seed), 6)
    queries = draw_queries(jax.random.fold_in(arg_keys[5], 71), 0)
    keys = draw_keys(jax.random.fold_in(arg_keys[5], 71), 0)
    values = bell_draw(arg_keys[2], (CTX_TOK, KVH * HD), 1.0, 6.0, ((0, 64), (1, 4)))
    stretch_lengths = ragged(arg_keys[3], NCH, CTX_TOK, TOK_DEV, 1).astype(jnp.int32)
    query_pos = jax.random.permutation(arg_keys[4], NQ).astype(jnp.int32)
    return {"queries": queries, "keys": keys, "values": values, "stretch_lengths": stretch_lengths, "query_pos": query_pos}


ROPE_BASE = 1000000.0
floor_value = -1e30


def rope_queries(queries, query_pos):
    query_count = queries.shape[0]
    head_count = queries.shape[1] // HD
    half_dim = HD // 2
    frequency = ROPE_BASE ** (-(jnp.arange(half_dim, dtype=jnp.float32) * 2.0 / HD))
    angles = query_pos.astype(jnp.float32)[:, None] * frequency[None, :]
    cosine = jnp.cos(angles)[:, None, :]
    sin_part = jnp.sin(angles)[:, None, :]
    as_float = queries.astype(jnp.float32).reshape(query_count, head_count, HD)
    front_half = as_float[..., :half_dim]
    back_half = as_float[..., half_dim:]
    rotated = jnp.concatenate([front_half * cosine - back_half * sin_part, back_half * cosine + front_half * sin_part], axis=-1)
    return rotated.astype(jnp.bfloat16)


def reference(queries, keys, values, stretch_lengths, query_pos):
    roped = rope_queries(queries, query_pos)
    group_size = HQ // KVH
    query_heads = roped.reshape(NQ, KVH, group_size, HD).transpose(1, 2, 0, 3)
    key_heads = keys.reshape(CTX_TOK, KVH, HD).transpose(1, 0, 2)
    value_heads = values.reshape(CTX_TOK, KVH, HD).transpose(1, 0, 2)
    starts = jnp.cumsum(stretch_lengths) - stretch_lengths
    stretch_ends = starts + stretch_lengths
    key_block_len = math.gcd(CTX_TOK, 8192)
    block_count = CTX_TOK // key_block_len
    score_scale = HD ** -0.5

    def one_head(pieces):
        q_group, k_group, v_group = pieces
        q_float = q_group.astype(jnp.float32)
        key_blocks = k_group.reshape(block_count, key_block_len, HD)
        value_blocks = v_group.reshape(block_count, key_block_len, HD)

        def score_block(k_block):
            return jnp.einsum('jqd,kd->jqk', q_float, k_block.astype(jnp.float32)) * score_scale

        def first_pass(state_pair, k_block):
            row_top, row_sum = state_pair
            logits = score_block(k_block)
            new_top = jnp.maximum(row_top, logits.max(-1))
            row_sum = row_sum * jnp.exp(row_top - new_top) + jnp.sum(jnp.exp(logits - new_top[..., None]), axis=-1)
            return (new_top, row_sum), None

        start_top = jnp.full((group_size, NQ), floor_value, jnp.float32)
        start_sum = jnp.zeros((group_size, NQ), jnp.float32)
        (row_top, row_sum), _ = lax.scan(first_pass, (start_top, start_sum), key_blocks)

        def second_pass(state_pair, pieces_two):
            weighted, mass_sum = state_pair
            k_block, v_block, block_index = pieces_two
            logits = score_block(k_block)
            rounded = jnp.exp(logits - row_top[..., None]).astype(jnp.bfloat16).astype(jnp.float32)
            weighted = weighted + jnp.einsum('jqk,kd->jqd', rounded, v_block.astype(jnp.float32))
            share = jnp.sum(rounded / row_sum[..., None], axis=0)
            key_position = block_index * key_block_len + jnp.arange(key_block_len, dtype=jnp.int32)
            onehot = ((key_position[:, None] >= starts[None, :]) & (key_position[:, None] < stretch_ends[None, :])).astype(jnp.float32)
            mass_sum = mass_sum + jnp.dot(share, onehot, precision=lax.Precision.HIGHEST)
            return (weighted, mass_sum), None

        start_weighted = jnp.zeros((group_size, NQ, HD), jnp.float32)
        start_mass = jnp.zeros((NQ, NCH), jnp.float32)
        block_ids = jnp.arange(block_count, dtype=jnp.int32)
        (weighted, mass_sum), _ = lax.scan(second_pass, (start_weighted, start_mass), (key_blocks, value_blocks, block_ids))
        return weighted / row_sum[..., None], mass_sum

    head_outputs, head_masses = lax.map(one_head, (query_heads, key_heads, value_heads))
    attended = head_outputs.transpose(2, 0, 1, 3).reshape(NQ, HQ * HD).astype(jnp.bfloat16)
    stretch_mass = (jnp.sum(head_masses, axis=0) * (NCH / HQ)).T
    return attended, stretch_mass
```

```python
import functools
import math

import jax
import jax.numpy as jnp
import numpy as np
from jax import lax
from jax.experimental import pallas as pl
from jax.experimental.pallas import tpu as pltpu
from jax.sharding import PartitionSpec as P

HD = 128
HALF = HD // 2
ROPE_BASE = 1000000.0
MESH = pl.DeviceIdType.MESH
NX, NY, NZ, NC = 4, 4, 8, 2
NQ = 512
TOK = 512
NCH = 256
HEADS = 10
KV = 2
GROUP = HEADS // KV
ROWS = NQ // (NX * NZ * NC)
LSE_ROWS = 16
HALF_Q = NQ // NC
MASS_ROWS = NCH // (NC * NY * NX)
GW = GROUP * HD


def kernel(
    q_ref, k_ref, v_ref, len_ref, pos_ref, freq_ref, att_ref, mass_ref,
    tab, w_mat, ot, mh, tops, lse, lse_in, lsx, lsx_in, lsz, lsz_in, lsg, lsg_in,
    osum, oc_in, ofar_in, onear_in, oz_in,
    mpart, mc_in, my_in, mx_in, mz, mz_in, mfull,
    s_core, r_core, s_lx, r_lx, s_lz, r_lz, s_ox, r_ox, s_oz, r_oz,
    s_my, r_my, s_mx, r_mx, s_mz, r_mz, s_gx, r_gx, s_gy, r_gy,
):
    ctx = lax.axis_index("ctx")
    y = lax.axis_index("head")
    x = ctx // (NZ * NC)
    z = (ctx // NC) % NZ
    c = ctx % NC
    oc = 1 - c

    def at(xx, zz, cc, yy):
        return ((xx * NZ + zz) * NC + cc, yy)

    partner = at(x, z, oc, y)

    def xpeer(d):
        return at((x + d) % NX, z, c, y)

    def zpeer(d):
        return at(x, (z + d) % NZ, c, y)

    def ypeer(d):
        return at(x, z, c, (y + d) % NY)

    def send(src, dst, ssem, rsem, dev):
        copy = pltpu.make_async_remote_copy(
            src_ref=src, dst_ref=dst, send_sem=ssem, recv_sem=rsem,
            device_id=dev, device_id_type=MESH,
        )
        copy.start()
        return copy

    barrier = pltpu.get_barrier_semaphore()
    peers = [partner] + [xpeer(d) for d in range(1, NX)]
    peers += [zpeer(d) for d in range(1, NZ)] + [ypeer(d) for d in range(1, NY)]
    for dev in peers:
        pl.semaphore_signal(barrier, inc=1, device_id=dev, device_id_type=MESH)

    angles = freq_ref[:, :1] * pos_ref[...].astype(jnp.float32)
    cosine = jnp.cos(angles).T
    sine = jnp.sin(angles).T
    tab[0] = jnp.concatenate([cosine, cosine], axis=1)
    tab[1] = jnp.concatenate([-sine, sine], axis=1)

    lens = len_ref[...].astype(jnp.float32)
    row = lax.broadcasted_iota(jnp.int32, (NCH, NCH), 0)
    col = lax.broadcasted_iota(jnp.int32, (NCH, NCH), 1)
    starts = jnp.sum(jnp.where(col < row, lens, 0.0), axis=1, keepdims=True)
    ends = jnp.sum(jnp.where(col <= row, lens, 0.0), axis=1, keepdims=True)
    token = (lax.broadcasted_iota(jnp.int32, (NCH, TOK), 1) + ctx * TOK).astype(jnp.float32)
    member = jnp.where((token >= starts) & (token < ends), 1.0, 0.0).astype(jnp.bfloat16)
    for g in range(KV):
        w_mat[g, HD:, :] = member
        w_mat[g, :HD, :] = v_ref[:, g * HD : (g + 1) * HD].astype(jnp.float32).T.astype(jnp.bfloat16)

    scale = HD ** -0.5
    exp_scale = scale * math.log2(math.e)
    lse[...] = jnp.zeros_like(lse)
    tops[...] = jnp.zeros_like(tops)

    for g in range(KV):

        def head(j, carry):
            h = g * GROUP + j
            cols = pl.ds(pl.multiple_of(h * HD, HD), HD)
            qh = q_ref[:, cols].astype(jnp.float32)
            roped = (qh * tab[0] + pltpu.roll(qh, HALF, 1) * tab[1]).astype(jnp.bfloat16)
            s = lax.dot_general(
                k_ref[:, g * HD : (g + 1) * HD], roped, (((1,), (1,)), ((), ())),
                preferred_element_type=jnp.float32,
            )
            top = jnp.max(s, axis=0, keepdims=True)
            p = jnp.exp2((s - top) * exp_scale)
            total = jnp.sum(p, axis=0, keepdims=True)
            both = jnp.dot(w_mat[g], p.astype(jnp.bfloat16), preferred_element_type=jnp.float32)
            ot[h] = both[:HD]
            mh[h] = both[HD:]
            tops[pl.ds(h, 1), :] = top * scale
            lse[pl.ds(h, 1), :] = top * scale + jnp.log(total)
            return carry

        lax.fori_loop(0, GROUP, head, 0)

    pl.semaphore_wait(barrier, len(peers))

    def merge(parts):
        top = functools.reduce(jnp.maximum, parts)
        return top + jnp.log(sum(jnp.exp(part - top) for part in parts))

    copy = send(lse, lse_in, s_core.at[0], r_core.at[0], partner)
    copy.wait()
    my_q = pl.ds(pl.multiple_of(c * HALF_Q, HALF_Q), HALF_Q)
    its_q = pl.ds(pl.multiple_of(oc * HALF_Q, HALF_Q), HALF_Q)
    lsx[...] = merge([lse[:, my_q], lse_in[:, my_q]])
    copies = [send(lsx, lsx_in.at[d - 1], s_lx.at[d - 1], r_lx.at[d - 1], xpeer(d)) for d in range(1, NX)]
    for copy in copies:
        copy.wait()
    lsz[...] = merge([lsx[...]] + [lsx_in[d] for d in range(NX - 1)])
    copies = [send(lsz, lsz_in.at[d - 1], s_lz.at[d - 1], r_lz.at[d - 1], zpeer(d)) for d in range(1, NZ)]
    for copy in copies:
        copy.wait()
    lsg[...] = merge([lsz[...]] + [lsz_in[d] for d in range(NZ - 1)])
    copy = send(lsg, lsg_in, s_core.at[1], r_core.at[1], partner)
    copy.wait()
    own_w = jnp.exp(tops[:, my_q] - lsg[...])
    its_w = jnp.exp(tops[:, its_q] - lsg_in[...])
    tops[:, my_q] = own_w
    tops[:, its_q] = its_w

    factor = NCH / (HEADS * NY)
    for cc in range(NC):
        for yy in range(NY):
            base = (cc * NY + yy) * NX * MASS_ROWS
            block = sum(
                mh[h, base : base + NX * MASS_ROWS, :] * tops[h : h + 1, :] for h in range(HEADS)
            )
            mpart[cc, yy] = (block * factor).reshape(NX, MASS_ROWS, NQ)
    m_core = send(mpart.at[oc], mc_in, s_core.at[2], r_core.at[2], partner)

    for h in range(HEADS):
        g, j = h // GROUP, h % GROUP
        turned = (ot[h] * tops[h : h + 1, :]).T.reshape(NX, NZ, NC, ROWS, HD)
        for cc in range(NC):
            osum[cc, g, :, :, :, j * HD : (j + 1) * HD] = turned[:, :, cc]
    o_core = send(osum.at[oc], oc_in, s_core.at[3], r_core.at[3], partner)

    m_core.wait()
    mc_in[...] = mc_in[...] + mpart[c]
    my_copies = [
        send(mc_in.at[(y + d) % NY], my_in.at[d - 1], s_my.at[d - 1], r_my.at[d - 1], ypeer(d))
        for d in range(1, NY)
    ]

    o_core.wait()
    far = (x + 2) % NX
    right = (x + 1) % NX
    left = (x + 3) % NX
    for g in range(KV):
        oc_in[g] = oc_in[g] + osum[c, g]
    ox_copies = [
        send(oc_in.at[0, far], ofar_in.at[0], s_ox.at[0], r_ox.at[0], xpeer(1)),
        send(oc_in.at[1, far], ofar_in.at[1], s_ox.at[1], r_ox.at[1], xpeer(3)),
        send(oc_in.at[1, right], onear_in.at[0, 1], s_ox.at[2], r_ox.at[2], xpeer(1)),
        send(oc_in.at[0, left], onear_in.at[1, 0], s_ox.at[3], r_ox.at[3], xpeer(3)),
    ]

    for copy in my_copies:
        copy.wait()
    mx = mc_in.at[y]
    mx[...] = mc_in[y] + my_in[0] + my_in[1] + my_in[2]
    mx_copies = [
        send(mc_in.at[y, (x + d) % NX], mx_in.at[d - 1], s_mx.at[d - 1], r_mx.at[d - 1], xpeer(d))
        for d in range(1, NX)
    ]

    ox_copies[0].wait()
    oc_in[0, right] = oc_in[0, right] + ofar_in[0]
    ox_copies.append(send(oc_in.at[0, right], onear_in.at[0, 0], s_ox.at[4], r_ox.at[4], xpeer(1)))
    ox_copies[1].wait()
    oc_in[1, left] = oc_in[1, left] + ofar_in[1]
    ox_copies.append(send(oc_in.at[1, left], onear_in.at[1, 1], s_ox.at[5], r_ox.at[5], xpeer(3)))

    for copy in mx_copies:
        copy.wait()
    mz[...] = mc_in[y, x] + mx_in[0] + mx_in[1] + mx_in[2]
    mz_copies = [send(mz, mz_in.at[d - 1], s_mz.at[d - 1], r_mz.at[d - 1], zpeer(d)) for d in range(1, NZ)]

    for copy in ox_copies[2:]:
        copy.wait()
    for g in range(KV):
        oc_in[g, x] = oc_in[g, x] + onear_in[0, g] + onear_in[1, g]
    oz_copies = [
        send(oc_in.at[:, x, (z + d) % NZ], oz_in.at[d - 1], s_oz.at[d - 1], r_oz.at[d - 1], zpeer(d))
        for d in range(1, NZ)
    ]

    for copy in mz_copies:
        copy.wait()
    mfull[c, y, x] = functools.reduce(jnp.add, [mz_in[d] for d in range(NZ - 1)], mz[...])
    gx_copies = [
        send(mfull.at[c, y, x], mfull.at[c, y, x], s_gx.at[d - 1], r_gx.at[d - 1], xpeer(d))
        for d in range(1, NX)
    ]
    for copy in gx_copies:
        copy.wait()
    gy_copies = [
        send(mfull.at[c, y], mfull.at[c, y], s_gy.at[d - 1], r_gy.at[d - 1], ypeer(d))
        for d in range(1, NY)
    ]
    for copy in gy_copies:
        copy.wait()
    m_back = send(mfull.at[c], mfull.at[c], s_core.at[4], r_core.at[4], partner)

    for copy in oz_copies:
        copy.wait()
    for g in range(KV):
        out = functools.reduce(jnp.add, [oz_in[d, g] for d in range(NZ - 1)], oc_in[g, x, z])
        att_ref[:, g * GW : (g + 1) * GW] = out.astype(jnp.bfloat16)
    m_back.wait()
    mass_ref[...] = mfull[...].reshape(NCH, NQ)


def local(queries, keys, values, stretch_lengths, query_pos):
    freq = (ROPE_BASE ** (-(np.arange(HALF, dtype=np.float64) * 2.0 / HD))).astype(np.float32)
    freq = jnp.asarray(np.broadcast_to(freq[:, None], (HALF, HD)))
    f32, bf16 = jnp.float32, jnp.bfloat16
    vmem, dma = pltpu.VMEM, pltpu.SemaphoreType.DMA
    return pl.pallas_call(
        kernel,
        out_shape=(
            jax.ShapeDtypeStruct((ROWS, HEADS * HD), bf16),
            jax.ShapeDtypeStruct((NCH, NQ), f32),
        ),
        in_specs=[pl.BlockSpec(memory_space=pltpu.VMEM)] * 6,
        out_specs=[pl.BlockSpec(memory_space=pltpu.VMEM)] * 2,
        scratch_shapes=[
            vmem((2, NQ, HD), f32),
            vmem((KV, HD + NCH, TOK), bf16),
            vmem((HEADS, HD, NQ), f32),
            vmem((HEADS, NCH, NQ), f32),
            vmem((LSE_ROWS, NQ), f32),
            vmem((LSE_ROWS, NQ), f32),
            vmem((LSE_ROWS, NQ), f32),
            vmem((LSE_ROWS, HALF_Q), f32),
            vmem((NX - 1, LSE_ROWS, HALF_Q), f32),
            vmem((LSE_ROWS, HALF_Q), f32),
            vmem((NZ - 1, LSE_ROWS, HALF_Q), f32),
            vmem((LSE_ROWS, HALF_Q), f32),
            vmem((LSE_ROWS, HALF_Q), f32),
            vmem((NC, KV, NX, NZ, ROWS, GW), f32),
            vmem((KV, NX, NZ, ROWS, GW), f32),
            vmem((2, NZ, ROWS, GW), f32),
            vmem((2, KV, NZ, ROWS, GW), f32),
            vmem((NZ - 1, KV, ROWS, GW), f32),
            vmem((NC, NY, NX, MASS_ROWS, NQ), f32),
            vmem((NY, NX, MASS_ROWS, NQ), f32),
            vmem((NY - 1, NX, MASS_ROWS, NQ), f32),
            vmem((NX - 1, MASS_ROWS, NQ), f32),
            vmem((MASS_ROWS, NQ), f32),
            vmem((NZ - 1, MASS_ROWS, NQ), f32),
            vmem((NC, NY, NX, MASS_ROWS, NQ), f32),
            dma((5,)), dma((5,)),
            dma((NX - 1,)), dma((NX - 1,)),
            dma((NZ - 1,)), dma((NZ - 1,)),
            dma((6,)), dma((6,)),
            dma((NZ - 1,)), dma((NZ - 1,)),
            dma((NY - 1,)), dma((NY - 1,)),
            dma((NX - 1,)), dma((NX - 1,)),
            dma((NZ - 1,)), dma((NZ - 1,)),
            dma((NX - 1,)), dma((NX - 1,)),
            dma((NY - 1,)), dma((NY - 1,)),
        ],
        compiler_params=pltpu.CompilerParams(
            collective_id=0, has_side_effects=True, vmem_limit_bytes=60 * 1024 * 1024
        ),
    )(queries, keys, values, stretch_lengths.reshape(1, NCH), query_pos.reshape(1, NQ), freq)


def solution(mesh):
    placed = (P(None, "head"), P("ctx", "head"), P("ctx", "head"), P(), P())
    return jax.shard_map(
        local, mesh=mesh, in_specs=placed, out_specs=(P("ctx", "head"), P()), check_vma=False
    )
```

```python
import functools
import math

import jax
import jax.numpy as jnp
import numpy as np
from jax import lax
from jax.experimental import pallas as pl
from jax.experimental.pallas import tpu as pltpu
from jax.sharding import PartitionSpec as P

HD = 128
HALF = HD // 2
ROPE_BASE = 1000000.0
MESH = pl.DeviceIdType.MESH
NX, NY, NZ, NC = 4, 4, 8, 2
NQ = 512
TOK = 512
NCH = 256
HEADS = 10
KV = 2
GROUP = HEADS // KV
ROWS = NQ // (NX * NZ * NC)
CHIP_ROWS = ROWS * NC
PAD = 8
MASS_ROWS = NCH // (NC * NY * NX)
GW = GROUP * HD
XY = [(dx, dy) for dx in range(NX) for dy in range(NY) if dx or dy]
FREQ = [float(np.float32(ROPE_BASE ** (-2.0 * i / HD))) for i in range(HALF)]


def kernel(
    q_ref, k_ref, v_ref, len_ref, pos_ref, att_ref, mass_ref,
    tab, rp, keys, w_mat, kv_out, kv_in, ot, mh, tops, lse,
    lsx, lsx_in, lsz, lsz_in, osum, ofar_in, onear_in, oz_in, oc_out, oc_in,
    mpart, mc_in, mx_in, mz, mz_in, mfull,
    s_core, r_core, s_lx, r_lx, s_lz, r_lz, s_ox, r_ox, s_oz, r_oz,
    s_mx, r_mx, s_mz, r_mz, s_gx, r_gx,
):
    ctx = lax.axis_index("ctx")
    y = lax.axis_index("head")
    x = ctx // (NZ * NC)
    z = (ctx // NC) % NZ
    c = ctx % NC
    oc = 1 - c

    def at(xx, zz, cc, yy):
        return ((xx * NZ + zz) * NC + cc, yy)

    partner = at(x, z, oc, y)

    def xpeer(d):
        return at((x + d) % NX, z, c, y)

    def zpeer(d):
        return at(x, (z + d) % NZ, c, y)

    def xypeer(dx, dy):
        return at((x + dx) % NX, z, c, (y + dy) % NY)

    def send(src, dst, ssem, rsem, dev):
        copy = pltpu.make_async_remote_copy(
            src_ref=src, dst_ref=dst, send_sem=ssem, recv_sem=rsem,
            device_id=dev, device_id_type=MESH,
        )
        copy.start()
        return copy

    barrier = pltpu.get_barrier_semaphore()
    peers = [partner] + [zpeer(d) for d in range(1, NZ)] + [xypeer(dx, dy) for dx, dy in XY]
    for dev in peers:
        pl.semaphore_signal(barrier, inc=1, device_id=dev, device_id_type=MESH)

    mine = pl.ds(pl.multiple_of(c * HD, HD), HD)
    other = pl.ds(pl.multiple_of(oc * HD, HD), HD)
    kv_out[0] = k_ref[:, other].astype(jnp.float32)
    kv_out[1] = v_ref[:, other].astype(jnp.float32)
    keys[0] = k_ref[:, mine]

    freq_row = lax.broadcasted_iota(jnp.int32, (HALF, HD), 0)
    freq = jnp.zeros((HALF, HD), jnp.float32)
    for i in range(HALF):
        freq = jnp.where(freq_row == i, FREQ[i], freq)
    angles = freq[:, :1] * pos_ref[...].astype(jnp.float32)
    cosine = jnp.cos(angles).T
    sine = jnp.sin(angles).T
    tab[0] = jnp.concatenate([cosine, cosine], axis=1)
    tab[1] = jnp.concatenate([-sine, sine], axis=1)

    lens = len_ref[...].astype(jnp.float32)
    row = lax.broadcasted_iota(jnp.int32, (NCH, NCH), 0)
    col = lax.broadcasted_iota(jnp.int32, (NCH, NCH), 1)
    starts = jnp.sum(jnp.where(col < row, lens, 0.0), axis=1, keepdims=True)
    ends = jnp.sum(jnp.where(col <= row, lens, 0.0), axis=1, keepdims=True)
    for half, shard in enumerate((ctx, ctx - c + oc)):
        token = (lax.broadcasted_iota(jnp.int32, (NCH, TOK), 1) + shard * TOK).astype(jnp.float32)
        member = jnp.where((token >= starts) & (token < ends), 1.0, 0.0).astype(jnp.bfloat16)
        w_mat[half, HD:, :] = member
    w_mat[0, :HD, :] = v_ref[:, mine].astype(jnp.float32).T.astype(jnp.bfloat16)

    scale = HD ** -0.5
    exp_scale = scale * math.log2(math.e)
    lse[...] = jnp.zeros_like(lse)
    tops[...] = jnp.zeros_like(tops)

    def rotate(j):
        cols = pl.ds(pl.multiple_of(c * GW + j * HD, HD), HD)
        qh = q_ref[:, cols].astype(jnp.float32)
        rp[j] = (qh * tab[0] + pltpu.roll(qh, HALF, 1) * tab[1]).astype(jnp.bfloat16)

    def attend(half, j):
        s = lax.dot_general(
            keys[half], rp[j], (((1,), (1,)), ((), ())), preferred_element_type=jnp.float32
        )
        top = jnp.max(s, axis=0, keepdims=True)
        p = jnp.exp2((s - top) * exp_scale)
        total = jnp.sum(p, axis=0, keepdims=True)
        both = jnp.dot(w_mat[half], p.astype(jnp.bfloat16), preferred_element_type=jnp.float32)
        ot[half, j] = both[:HD]
        mh[half, j] = both[HD:]
        tops[half, pl.ds(j, 1), :] = top * scale
        lse[half, pl.ds(j, 1), :] = top * scale + jnp.log(total)

    def first(j, carry):
        rotate(j)
        attend(0, j)
        return carry

    def second(j, carry):
        attend(1, j)
        return carry

    early = 3
    lax.fori_loop(0, early, first, 0)
    pl.semaphore_wait(barrier, len(peers))
    kv_copy = send(kv_out, kv_in, s_core.at[0], r_core.at[0], partner)
    lax.fori_loop(early, GROUP, first, 0)
    kv_copy.wait()
    keys[1] = kv_in[0].astype(jnp.bfloat16)
    w_mat[1, :HD, :] = kv_in[1].T.astype(jnp.bfloat16)
    lax.fori_loop(0, GROUP, second, 0)

    def merge(parts):
        top = functools.reduce(jnp.maximum, parts)
        return top + jnp.log(sum(jnp.exp(part - top) for part in parts))

    lsx[...] = merge([lse[0], lse[1]])
    lx_copies = [send(lsx, lsx_in.at[d - 1], s_lx.at[d - 1], r_lx.at[d - 1], xpeer(d)) for d in range(1, NX)]
    for copy in lx_copies:
        copy.wait()
    lsz[...] = merge([lsx[...]] + [lsx_in[d] for d in range(NX - 1)])
    lz_copies = [send(lsz, lsz_in.at[d - 1], s_lz.at[d - 1], r_lz.at[d - 1], zpeer(d)) for d in range(1, NZ)]

    scales = [jnp.exp(tops[half] - lsz[...]) for half in range(NC)]
    for j in range(GROUP):
        turned = ot[0, j] * scales[0][j : j + 1, :] + ot[1, j] * scales[1][j : j + 1, :]
        osum[:, :, :, j * HD : (j + 1) * HD] = turned.T.reshape(NX, NZ, CHIP_ROWS, HD)
    far = (x + 2) % NX
    right = (x + 1) % NX
    left = (x + 3) % NX
    low, high = pl.ds(0, NZ // 2), pl.ds(NZ // 2, NZ // 2)
    ox_copies = [
        send(osum.at[far, low], ofar_in.at[0], s_ox.at[0], r_ox.at[0], xpeer(1)),
        send(osum.at[far, high], ofar_in.at[1], s_ox.at[1], r_ox.at[1], xpeer(3)),
        send(osum.at[right, high], onear_in.at[0, high], s_ox.at[2], r_ox.at[2], xpeer(1)),
        send(osum.at[left, low], onear_in.at[1, low], s_ox.at[3], r_ox.at[3], xpeer(3)),
    ]

    for copy in lz_copies:
        copy.wait()
    whole = merge([lsz[...]] + [lsz_in[d] for d in range(NZ - 1)])

    factor = NCH / (HEADS * NY)
    weights = [jnp.exp(tops[half] - whole) * factor for half in range(NC)]
    for cc in range(NC):
        for xx in range(NX):
            base = (cc * NX + xx) * NY * MASS_ROWS
            block = sum(
                mh[half, j, base : base + NY * MASS_ROWS, :] * weights[half][j : j + 1, :]
                for half in range(NC)
                for j in range(GROUP)
            )
            mpart[cc, xx] = block.reshape(NY, MASS_ROWS, NQ)
    m_core = send(mpart.at[oc], mc_in, s_core.at[1], r_core.at[1], partner)
    lsz[...] = jnp.exp(lsz[...] - whole)
    m_core.wait()
    mc_in[...] = mc_in[...] + mpart[c]
    mx_copies = [
        send(
            mc_in.at[(x + dx) % NX, (y + dy) % NY], mx_in.at[i], s_mx.at[i], r_mx.at[i],
            xypeer(dx, dy),
        )
        for i, (dx, dy) in enumerate(XY)
    ]

    ox_copies[0].wait()
    osum[right, low] = osum[right, low] + ofar_in[0]
    ox_copies.append(send(osum.at[right, low], onear_in.at[0, low], s_ox.at[4], r_ox.at[4], xpeer(1)))
    ox_copies[1].wait()
    osum[left, high] = osum[left, high] + ofar_in[1]
    ox_copies.append(send(osum.at[left, high], onear_in.at[1, high], s_ox.at[5], r_ox.at[5], xpeer(3)))

    for copy in mx_copies:
        copy.wait()
    mz[...] = functools.reduce(jnp.add, [mx_in[i] for i in range(len(XY))], mc_in[x, y])
    mz_copies = [send(mz, mz_in.at[d - 1], s_mz.at[d - 1], r_mz.at[d - 1], zpeer(d)) for d in range(1, NZ)]

    for copy in ox_copies[2:]:
        copy.wait()
    change = lsz[:, pl.ds(pl.multiple_of(x * HD, HD), HD)].T
    for zz in range(NZ):
        rows = change[zz * CHIP_ROWS : (zz + 1) * CHIP_ROWS]
        for j in range(GROUP):
            cols = slice(j * HD, (j + 1) * HD)
            osum[x, zz, :, cols] = (
                osum[x, zz, :, cols] + onear_in[0, zz, :, cols] + onear_in[1, zz, :, cols]
            ) * rows[:, j : j + 1]
    oz_copies = [
        send(osum.at[x, (z + d) % NZ], oz_in.at[d - 1], s_oz.at[d - 1], r_oz.at[d - 1], zpeer(d))
        for d in range(1, NZ)
    ]

    for copy in mz_copies:
        copy.wait()
    mfull[c, x, y] = functools.reduce(jnp.add, [mz_in[d] for d in range(NZ - 1)], mz[...])
    gx_copies = [
        send(mfull.at[c, x, y], mfull.at[c, x, y], s_gx.at[i], r_gx.at[i], xypeer(dx, dy))
        for i, (dx, dy) in enumerate(XY)
    ]

    for copy in oz_copies:
        copy.wait()
    oc_out[...] = functools.reduce(
        jnp.add, [oz_in[d] for d in range(NZ - 1)], osum[x, z]
    ).reshape(NC, ROWS, GW)
    o_core = send(oc_out.at[oc], oc_in, s_core.at[2], r_core.at[2], partner)

    for copy in gx_copies:
        copy.wait()
    m_back = send(mfull.at[c], mfull.at[c], s_core.at[3], r_core.at[3], partner)
    o_core.wait()
    own, received = oc_out[c], oc_in[...]
    att_ref[:, :GW] = jnp.where(c == 0, own, received).astype(jnp.bfloat16)
    att_ref[:, GW:] = jnp.where(c == 0, received, own).astype(jnp.bfloat16)
    m_back.wait()
    mass_ref[...] = mfull[...].reshape(NCH, NQ)


def local(queries, keys, values, stretch_lengths, query_pos):
    f32, bf16 = jnp.float32, jnp.bfloat16
    vmem, dma = pltpu.VMEM, pltpu.SemaphoreType.DMA
    return pl.pallas_call(
        kernel,
        out_shape=(
            jax.ShapeDtypeStruct((ROWS, HEADS * HD), bf16),
            jax.ShapeDtypeStruct((NCH, NQ), f32),
        ),
        in_specs=[pl.BlockSpec(memory_space=pltpu.VMEM)] * 5,
        out_specs=[pl.BlockSpec(memory_space=pltpu.VMEM)] * 2,
        scratch_shapes=[
            vmem((2, NQ, HD), f32),
            vmem((GROUP, NQ, HD), bf16),
            vmem((NC, TOK, HD), bf16),
            vmem((NC, HD + NCH, TOK), bf16),
            vmem((2, TOK, HD), f32),
            vmem((2, TOK, HD), f32),
            vmem((NC, GROUP, HD, NQ), f32),
            vmem((NC, GROUP, NCH, NQ), f32),
            vmem((NC, PAD, NQ), f32),
            vmem((NC, PAD, NQ), f32),
            vmem((PAD, NQ), f32),
            vmem((NX - 1, PAD, NQ), f32),
            vmem((PAD, NQ), f32),
            vmem((NZ - 1, PAD, NQ), f32),
            vmem((NX, NZ, CHIP_ROWS, GW), f32),
            vmem((2, NZ // 2, CHIP_ROWS, GW), f32),
            vmem((2, NZ, CHIP_ROWS, GW), f32),
            vmem((NZ - 1, CHIP_ROWS, GW), f32),
            vmem((NC, ROWS, GW), f32),
            vmem((ROWS, GW), f32),
            vmem((NC, NX, NY, MASS_ROWS, NQ), f32),
            vmem((NX, NY, MASS_ROWS, NQ), f32),
            vmem((len(XY), MASS_ROWS, NQ), f32),
            vmem((MASS_ROWS, NQ), f32),
            vmem((NZ - 1, MASS_ROWS, NQ), f32),
            vmem((NC, NX, NY, MASS_ROWS, NQ), f32),
            dma((4,)), dma((4,)),
            dma((NX - 1,)), dma((NX - 1,)),
            dma((NZ - 1,)), dma((NZ - 1,)),
            dma((6,)), dma((6,)),
            dma((NZ - 1,)), dma((NZ - 1,)),
            dma((len(XY),)), dma((len(XY),)),
            dma((NZ - 1,)), dma((NZ - 1,)),
            dma((len(XY),)), dma((len(XY),)),
        ],
        compiler_params=pltpu.CompilerParams(
            collective_id=0, has_side_effects=True, vmem_limit_bytes=60 * 1024 * 1024
        ),
    )(queries, keys, values, stretch_lengths.reshape(1, NCH), query_pos.reshape(1, NQ))


def solution(mesh):
    placed = (P(None, "head"), P("ctx", "head"), P("ctx", "head"), P(), P())
    return jax.shard_map(
        local, mesh=mesh, in_specs=placed, out_specs=(P("ctx", "head"), P()), check_vma=False
    )
```
